512 devices in a mesh: section: 8 (over y_hi, x), head: 4 (over y_lo, core), tok: 16 (over z).
Axes of the slice: x: 4, y: 4 (y_hi: 2, y_lo: 2; y = y_hi * 2 + y_lo), z: 16, core: 2. Of those that a mesh axis runs over, the one named last changes fastest.
Arguments:
- held_cotangents: bfloat16 [8, 2, 2048, 2560], P('section', None, 'tok', 'head'), may hold values from -6 to 6
- entering_adjoint: bfloat16 [2048, 2560], P('tok', 'head'), may hold values from -6 to 6
- saved_queries: bfloat16 [8, 2048, 2560], P('section', 'tok', 'head'), may hold values from -1024 to 1024
- saved_keys: bfloat16 [8, 2048, 2560], P('section', 'tok', 'head'), may hold values from -20 to 20
- value_weight: bfloat16 [8, 2560, 2560], P('section', None, 'head'), may hold values from -0.125 to 0.125
- out_weight: bfloat16 [8, 2560, 2560], P('section', 'tok', 'head'), may hold values from -0.125 to 0.125
- block_gate: float32 [8, 2560], P('section'), may hold values from -3 to 3
- time_gate: float32 [32, 2560], replicated, may hold values from -3 to 3
- timestep: int32 [1], replicated, may hold values from 0 to 31
Outputs:
- passed: bfloat16 [8, 2, 2048, 2560], P('section', None, 'tok', 'head')
The draws below stay inside these ranges and needn't reach their ends.
All inputs are finite; a program needn't handle non-finite values.
Results may differ from the reference program's by a relative error of at most 0.0085.
Values may be sent and summed in bfloat16 or wider, within the bound.
A program may use at most 64 MiB of HBM per device.

```python
import jax
import jax.numpy as jnp
from jax import lax

D = 2560
HEADS = 20
HD = 128
NSTEPS = 32
TOK_SH = 128
SECTIONS = 8
TOKENS = 2048
N_HEAD = 4
N_TOK = 16


def paired_rows(key):
    full_shape = (SECTIONS, TOKENS, HEADS, HD)
    query_vals = 1.6 * jax.random.truncated_normal(jax.random.fold_in(key, 101), -4.0, 4.0, full_shape)
    key_vals = 1.6 * jax.random.truncated_normal(jax.random.fold_in(key, 102), -4.0, 4.0, full_shape)
    return (query_vals.reshape(SECTIONS, TOKENS, HEADS * HD), key_vals.reshape(SECTIONS, TOKENS, HEADS * HD))


def draw_saved_queries(key, part):
    return paired_rows(key)[0].astype(jnp.bfloat16)


def draw_saved_keys(key, part):
    return paired_rows(key)[1].astype(jnp.bfloat16)


def block_scale(key, extent, split, low, high):
    level, own = 1.0, jax.random.fold_in(key, 6)
    for position, shards_of in split:
        draws = jnp.exp(jax.random.uniform(jax.random.fold_in(own, position), (shards_of,), jnp.float32, low / len(split), high / len(split)))
        level = level * jnp.repeat(draws, extent[position] // shards_of).reshape([-1 if axis == position else 1 for axis in range(len(extent))])
    return level


def gaussian(stream_key, dims, deviation, bound, shards=(), held_as=jnp.bfloat16):
    level = block_scale(stream_key, dims, shards, -0.22, 0.18) if shards else 1.0
    result = jax.random.normal(stream_key, dims, jnp.float32) * deviation * level
    return jnp.minimum(jnp.maximum(result, -bound), bound).astype(held_as)


def setup_inputs(seed: int = 0) -> dict:
    splits = jax.random.split(jax.random.key(seed), 10)
    held_cotangents = gaussian(splits[0], (SECTIONS, 2, TOKENS, D), 1.0, 6.0, ((0, 8), (2, 16), (3, 4)))
    entering_adjoint = gaussian(splits[1], (TOKENS, D), 1.0, 6.0, ((0, 16), (1, 4)))
    saved_queries = draw_saved_queries(jax.random.fold_in(splits[9], 71), 0)
    saved_keys = draw_saved_keys(jax.random.fold_in(splits[9], 71), 0)
    value_weight = gaussian(splits[4], (SECTIONS, D, HEADS * HD), D ** -0.5, 0.125, ((0, 8), (2, 4)))
    out_weight = gaussian(splits[5], (SECTIONS, D, HEADS * HD), (HEADS * HD) ** -0.5, 0.125, ((0, 8), (1, 16), (2, 4)))
    block_gate = gaussian(splits[6], (SECTIONS, D), 0.6, 3.0, ((0, 8),), jnp.float32)
    time_gate = gaussian(splits[7], (NSTEPS, D), 0.6, 3.0, (), jnp.float32)
    timestep = jax.random.randint(splits[8], (1,), 0, NSTEPS).astype(jnp.int32)
    return {"held_cotangents": held_cotangents, "entering_adjoint": entering_adjoint, "saved_queries": saved_queries, "saved_keys": saved_keys, "value_weight": value_weight, "out_weight": out_weight, "block_gate": block_gate, "time_gate": time_gate, "timestep": timestep}


GUIDE = 3.0

def section_vjp(inputs):
    held_section, query_section, key_section, value_section, output_section, gate_row = inputs
    rows_all = held_section.shape[1]
    width = held_section.shape[2]
    scaled = (held_section.astype(jnp.float32) * gate_row).astype(jnp.bfloat16)
    attn_grad = jnp.dot(scaled.reshape(2 * rows_all, width), output_section, preferred_element_type=jnp.float32)
    attn_grad = attn_grad.astype(jnp.bfloat16).reshape(2, rows_all, HEADS * HD)
    query_heads = jnp.transpose(query_section.reshape(rows_all, HEADS, HD), (1, 0, 2))
    key_heads = jnp.transpose(key_section.reshape(rows_all, HEADS, HD), (1, 0, 2))
    grad_heads = jnp.transpose(attn_grad[0].reshape(rows_all, HEADS, HD), (1, 0, 2))

    def one_head(head_inputs):
        query_one, key_one, grad_one = head_inputs
        scores = jnp.dot(query_one, key_one.T, preferred_element_type=jnp.float32) * HD ** (-0.5)
        row_top = lax.optimization_barrier(jnp.max(scores, axis=1, keepdims=True))
        log_total = row_top + jnp.log(lax.optimization_barrier(jnp.sum(jnp.exp(scores - row_top), axis=1, keepdims=True)))
        weights = jnp.exp(scores - log_total).astype(jnp.bfloat16)
        blocked = jnp.einsum('bij,bie->bje', weights.reshape(N_TOK, TOK_SH, rows_all).astype(jnp.float32), grad_one.reshape(N_TOK, TOK_SH, HD).astype(jnp.float32), precision=lax.Precision.HIGHEST)
        blocked = lax.optimization_barrier(blocked.astype(jnp.bfloat16))
        return lax.optimization_barrier(jnp.sum(blocked.astype(jnp.float32), axis=0)).astype(jnp.bfloat16)
    normal_value = lax.map(one_head, (query_heads, key_heads, grad_heads))
    normal_value = jnp.transpose(normal_value, (1, 0, 2)).reshape(rows_all, HEADS * HD)
    value_grad = jnp.stack([normal_value, attn_grad[1]])
    group_width = HEADS * HD // N_HEAD
    back_sum = jnp.zeros((2 * rows_all, width), jnp.float32)
    for group_index in range(N_HEAD):
        lower = group_index * group_width
        upper_col = lower + group_width
        partial_value = jnp.dot(value_grad[:, :, lower:upper_col].reshape(2 * rows_all, group_width), value_section[:, lower:upper_col].T, preferred_element_type=jnp.float32)
        partial_value = lax.optimization_barrier(partial_value.astype(jnp.bfloat16))
        back_sum = back_sum + partial_value.astype(jnp.float32)
    return (held_section.astype(jnp.float32) + back_sum.reshape(2, rows_all, width)).astype(jnp.bfloat16)

def reference(held_cotangents, entering_adjoint, saved_queries, saved_keys, value_weight, out_weight, block_gate, time_gate, timestep):
    step_ids = jnp.arange(NSTEPS).astype(jnp.int32)
    time_row = lax.optimization_barrier(jnp.sum(jnp.where((step_ids == timestep[0])[:, None], time_gate, jnp.zeros_like(time_gate)), axis=0))
    gates = block_gate + time_row[None, :]
    block_cots = lax.map(section_vjp, (held_cotangents, saved_queries, saved_keys, value_weight, out_weight, gates))
    entering_full = entering_adjoint.astype(jnp.float32)
    fresh_rows = jnp.stack([(1.0 + GUIDE) * entering_full, -GUIDE * entering_full]).astype(jnp.bfloat16)
    return jnp.concatenate([block_cots[1:], fresh_rows[None]], axis=0)
```

```python
import functools

import jax
import jax.numpy as jnp
from jax import lax
from jax.experimental import pallas as pl
from jax.experimental.pallas import tpu as pltpu
from jax.sharding import PartitionSpec as P

HD = 128
GUIDE = 3.0
MESH = pl.DeviceIdType.MESH
LOG2E = 1.4426950408889634
NT = (((1,), (1,)), ((), ()))
QCHUNK = 256


def kernel(
    n_sec,
    n_head,
    n_tok,
    held,
    qs,
    ks,
    vw,
    ow,
    bgate,
    tgate,
    tstep,
    out,
    held_v,
    scaled,
    w_full,
    v_full,
    q_all,
    k_all,
    g_all,
    probs,
    grad,
    o_buf,
    vgrad,
    part,
    part_in,
    cot,
    load_sem,
    a_send,
    a_recv,
    r_send,
    r_recv,
    q_send,
    q_recv,
    k_send,
    k_recv,
    g_send,
    g_recv,
    o_send,
    o_recv,
    p_send,
    p_recv,
    c_send,
    c_recv,
):
    sec, head, z = lax.axis_index("section"), lax.axis_index("head"), lax.axis_index("tok")
    core = lax.rem(head, 2)
    width = held.shape[3]
    rows = held.shape[2]
    heads_here = width // HD
    wrows = ow.shape[1]
    half_rows = wrows // 2
    right, left = lax.rem(z + 1, n_tok), lax.rem(z + n_tok - 1, n_tok)
    my_head = z // 3
    owner = jnp.logical_and(lax.rem(z, 3) == core, z < 3 * heads_here)

    def wblock(index, half):
        start = pl.multiple_of(index * wrows + half * half_rows, 16)
        return w_full.at[pl.ds(start, half_rows), :]

    load_held = pltpu.make_async_copy(held.at[0], held_v, load_sem.at[0])
    load_held.start()
    load_w = pltpu.make_async_copy(
        ow.at[0], w_full.at[pl.ds(pl.multiple_of(z * wrows, 16), wrows), :], load_sem.at[1]
    )
    load_w.start()
    load_v = pltpu.make_async_copy(vw.at[0], v_full, load_sem.at[2])
    load_v.start()

    barrier = pltpu.get_barrier_semaphore()
    for step in range(1, n_tok):
        pl.semaphore_signal(
            barrier, inc=1, device_id={"tok": lax.rem(z + step, n_tok)}, device_id_type=MESH
        )
    for step in range(1, n_head):
        pl.semaphore_signal(
            barrier, inc=1, device_id={"head": lax.rem(head + step, n_head)}, device_id_type=MESH
        )
    for step in (1, n_sec - 1):
        pl.semaphore_signal(
            barrier, inc=1, device_id={"section": lax.rem(sec + step, n_sec)}, device_id_type=MESH
        )
    pl.semaphore_wait(barrier, n_tok - 1 + n_head - 1 + 2)

    def ring(direction, half, step):
        block = lax.rem(z + n_tok - step, n_tok) if direction == 0 else lax.rem(z + step, n_tok)
        view = wblock(block, half)
        return pltpu.make_async_remote_copy(
            src_ref=view,
            dst_ref=view,
            send_sem=r_send.at[direction, half, step],
            recv_sem=r_recv.at[direction, half, step],
            device_id={"tok": right if direction == 0 else left},
            device_id_type=MESH,
        )

    load_w.wait()
    for half in (0, 1):
        for direction in (0, 1):
            ring(direction, half, 0).start()

    time_row = jnp.sum(
        jnp.where(
            lax.broadcasted_iota(jnp.int32, (tgate.shape[0], width), 0) == tstep[0],
            tgate[:, pl.ds(pl.multiple_of(head * width, 128), width)],
            0.0,
        ),
        axis=0,
        keepdims=True,
    )
    gate_row = bgate[:, pl.ds(pl.multiple_of(head * width, 128), width)] + time_row
    load_held.wait()
    for branch in (0, 1):
        scaled[head, branch * rows : (branch + 1) * rows, :] = (
            held_v[branch].astype(jnp.float32) * gate_row
        ).astype(jnp.bfloat16)

    def to_mate(step):
        return pltpu.make_async_remote_copy(
            src_ref=scaled.at[head],
            dst_ref=scaled.at[head],
            send_sem=a_send.at[step - 1],
            recv_sem=a_recv.at[step - 1],
            device_id={"head": lax.rem(head + step, n_head)},
            device_id_type=MESH,
        )

    for step in range(1, n_head):
        to_mate(step).start()

    def to_owner(source, target_ref, send_sem, recv_sem, index):
        owner_z = 3 * index + core

        @pl.when(owner_z == z)
        def _():
            pltpu.make_async_copy(source, target_ref.at[z], recv_sem).start()

        @pl.when(owner_z != z)
        def _():
            pltpu.make_async_remote_copy(
                src_ref=source,
                dst_ref=target_ref.at[z],
                send_sem=send_sem.at[index],
                recv_sem=recv_sem,
                device_id={"tok": owner_z},
                device_id_type=MESH,
            ).start()

    def wait_to_owner(source, target_ref, send_sem, recv_sem, index):
        owner_z = 3 * index + core

        @pl.when(owner_z != z)
        def _():
            pltpu.make_async_remote_copy(
                src_ref=source,
                dst_ref=target_ref.at[z],
                send_sem=send_sem.at[index],
                recv_sem=recv_sem,
                device_id={"tok": owner_z},
                device_id_type=MESH,
            ).wait_send()

    def head_cols(index):
        return slice(index * HD, (index + 1) * HD)

    for index in range(heads_here):
        to_owner(ks.at[0, :, head_cols(index)], k_all, k_send, k_recv, index)
        to_owner(qs.at[0, :, head_cols(index)], q_all, q_send, q_recv, index)

    chunks = n_tok * rows // QCHUNK
    per_chunk = QCHUNK // rows

    def weigh(chunk):
        query = q_all[pl.ds(chunk * per_chunk, per_chunk)].reshape(QCHUNK, HD)
        key = k_all[...].reshape(n_tok * rows, HD)
        raw = lax.dot_general(key, query, NT, preferred_element_type=jnp.float32) * (
            HD ** (-0.5) * LOG2E
        )
        top = jnp.max(raw, axis=0, keepdims=True)
        grown = jnp.exp2(raw - top)
        total = jnp.sum(grown, axis=0, keepdims=True)
        cols = pl.ds(pl.multiple_of(chunk * QCHUNK, QCHUNK), QCHUNK)
        probs[:, cols] = (grown * (1.0 / total)).astype(jnp.bfloat16)

    last = n_tok // 2 - 1
    first_weigh = last - chunks // 2 + 1

    def hop(step, sends):
        for half in (0, 1):
            for direction in (0, 1):
                ring(direction, half, step - 1).wait_recv()
                if (direction, half) in sends:
                    ring(direction, half, step).start()

    def weigh_at(step):
        @pl.when(jnp.logical_and(owner, step >= first_weigh))
        def _():
            @pl.when(step == first_weigh)
            def _():
                pltpu.make_async_copy(k_all, k_all, k_recv).wait()
                pltpu.make_async_copy(q_all, q_all, q_recv).wait()

            @pl.loop(0, 2)
            def _(turn):
                weigh((step - first_weigh) * 2 + turn)

    @pl.loop(1, last)
    def _(step):
        hop(step, ((0, 0), (0, 1), (1, 0), (1, 1)))
        weigh_at(step)

    hop(last, ((0, 0), (1, 1)))
    weigh_at(jnp.int32(last))
    for step in range(1, n_head):
        to_mate(step).wait_recv()
    ring(0, 0, last).wait_recv()
    ring(1, 1, last).wait_recv()

    for low in range(0, width, 2 * HD):
        high = min(low + 2 * HD, width)
        total = None
        for part_head in range(n_head):
            term = jnp.dot(
                scaled[part_head],
                w_full[part_head * width : (part_head + 1) * width, low:high],
                preferred_element_type=jnp.float32,
            )
            total = term if total is None else total + term
        for branch in (0, 1):
            grad[branch, :, low:high] = total[branch * rows : (branch + 1) * rows].astype(jnp.bfloat16)
        for index in range(low // HD, high // HD):
            to_owner(grad.at[0, :, head_cols(index)], g_all, g_send, g_recv, index)

    load_v.wait()

    def piece(branch, step):
        return pltpu.make_async_remote_copy(
            src_ref=part.at[branch, step],
            dst_ref=part_in.at[branch, step - 1],
            send_sem=p_send.at[branch, step - 1],
            recv_sem=p_recv.at[branch, step - 1],
            device_id={"head": lax.rem(head + step, n_head)},
            device_id_type=MESH,
        )

    def project(branch, value):
        for step in (2, 1, 3, 0):
            target = lax.rem(head + step, n_head)
            weight = v_full[pl.ds(pl.multiple_of(target * width, 128), width), :]
            part[branch, step] = lax.dot_general(
                value, weight, NT, preferred_element_type=jnp.float32
            ).astype(jnp.bfloat16)
            if step:
                piece(branch, step).start()

    def relay(branch):
        return pltpu.make_async_remote_copy(
            src_ref=cot.at[branch],
            dst_ref=out.at[branch],
            send_sem=c_send.at[branch],
            recv_sem=c_recv.at[branch],
            device_id={"section": lax.rem(sec + n_sec - 1, n_sec)},
            device_id_type=MESH,
        )

    def finish(branch):
        for step in range(1, n_head):
            piece(branch, step).wait_recv()
        back = part[branch, 0].astype(jnp.float32)
        for step in range(1, n_head):
            back = back + part_in[branch, step - 1].astype(jnp.float32)
        cot[branch] = (held_v[branch].astype(jnp.float32) + back).astype(jnp.bfloat16)
        relay(branch).start()

    project(1, grad[1])

    own_cols = pl.ds(pl.multiple_of(my_head * HD, HD), HD)

    def back_to(block):
        return pltpu.make_async_remote_copy(
            src_ref=o_buf.at[block],
            dst_ref=vgrad.at[:, own_cols],
            send_sem=o_send.at[block],
            recv_sem=o_recv,
            device_id={"tok": block},
            device_id_type=MESH,
        )

    @pl.when(owner)
    def _():
        pltpu.make_async_copy(g_all, g_all, g_recv).wait()

        @pl.loop(0, n_tok)
        def _(turn):
            block = lax.rem(z + n_tok // 2 + turn, n_tok)
            o_buf[block] = jnp.dot(
                probs[pl.ds(pl.multiple_of(block * rows, rows), rows), :],
                g_all[...].reshape(n_tok * rows, HD),
                preferred_element_type=jnp.float32,
            ).astype(jnp.bfloat16)

            @pl.when(block == z)
            def _():
                pltpu.make_async_copy(o_buf.at[block], vgrad.at[:, own_cols], o_recv).start()

            @pl.when(block != z)
            def _():
                back_to(block).start()

    finish(1)
    pltpu.make_async_copy(vgrad, vgrad, o_recv).wait()
    project(0, vgrad[...])
    finish(0)

    for index in range(heads_here):
        wait_to_owner(ks.at[0, :, head_cols(index)], k_all, k_send, k_recv, index)
        wait_to_owner(qs.at[0, :, head_cols(index)], q_all, q_send, q_recv, index)
        wait_to_owner(grad.at[0, :, head_cols(index)], g_all, g_send, g_recv, index)

    @pl.loop(0, last)
    def _(step):
        for half in (0, 1):
            for direction in (0, 1):
                ring(direction, half, step).wait_send()

    ring(0, 0, last).wait_send()
    ring(1, 1, last).wait_send()

    @pl.when(owner)
    def _():
        @pl.loop(0, n_tok)
        def _(block):
            @pl.when(block != z)
            def _():
                back_to(block).wait_send()

    for step in range(1, n_head):
        to_mate(step).wait_send()
        piece(0, step).wait_send()
        piece(1, step).wait_send()
    for branch in (1, 0):
        relay(branch).wait()


def shards(
    sizes,
    held_cotangents,
    entering_adjoint,
    saved_queries,
    saved_keys,
    value_weight,
    out_weight,
    block_gate,
    time_gate,
    timestep,
):
    n_sec, n_head, n_tok = sizes
    _, branches, rows, width = held_cotangents.shape
    heads_here = width // HD
    model = block_gate.shape[1]
    tokens = n_tok * rows
    bf16 = jnp.bfloat16
    dma = pltpu.SemaphoreType.DMA
    anywhere = pl.BlockSpec(memory_space=pl.ANY)
    vmem = pl.BlockSpec(memory_space=pltpu.VMEM)
    passed_on = pl.pallas_call(
        functools.partial(kernel, n_sec, n_head, n_tok),
        out_shape=jax.ShapeDtypeStruct((branches, rows, width), bf16),
        in_specs=[anywhere] * 5 + [vmem, vmem, pl.BlockSpec(memory_space=pltpu.SMEM)],
        out_specs=anywhere,
        scratch_shapes=[
            pltpu.VMEM((branches, rows, width), bf16),
            pltpu.VMEM((n_head, branches * rows, width), bf16),
            pltpu.VMEM((model, width), bf16),
            pltpu.VMEM((model, width), bf16),
            pltpu.VMEM((n_tok, rows, HD), bf16),
            pltpu.VMEM((n_tok, rows, HD), bf16),
            pltpu.VMEM((n_tok, rows, HD), bf16),
            pltpu.VMEM((tokens, tokens), bf16),
            pltpu.VMEM((branches, rows, width), bf16),
            pltpu.VMEM((n_tok, rows, HD), bf16),
            pltpu.VMEM((rows, width), bf16),
            pltpu.VMEM((branches, n_head, rows, width), bf16),
            pltpu.VMEM((branches, n_head - 1, rows, width), bf16),
            pltpu.VMEM((branches, rows, width), bf16),
            dma((3,)),
            dma((n_head - 1,)),
            dma((n_head - 1,)),
            dma((2, 2, n_tok // 2)),
            dma((2, 2, n_tok // 2)),
            dma((heads_here,)),
            dma,
            dma((heads_here,)),
            dma,
            dma((heads_here,)),
            dma,
            dma((n_tok,)),
            dma,
            dma((branches, n_head - 1)),
            dma((branches, n_head - 1)),
            dma((branches,)),
            dma((branches,)),
        ],
        compiler_params=pltpu.CompilerParams(
            collective_id=0, has_side_effects=True, vmem_limit_bytes=56 * 1024 * 1024
        ),
        name="tick",
    )(
        held_cotangents,
        saved_queries,
        saved_keys,
        value_weight,
        out_weight,
        block_gate,
        time_gate,
        timestep,
    )
    entering_full = entering_adjoint.astype(jnp.float32)
    fresh_rows = jnp.stack([(1.0 + GUIDE) * entering_full, -GUIDE * entering_full]).astype(bf16)
    is_last = lax.axis_index("section") == n_sec - 1
    return jnp.where(is_last, fresh_rows, passed_on)[None]


def solution(mesh):
    sizes = (mesh.shape["section"], mesh.shape["head"], mesh.shape["tok"])
    return jax.shard_map(
        functools.partial(shards, sizes),
        mesh=mesh,
        in_specs=(
            P("section", None, "tok", "head"),
            P("tok", "head"),
            P("section", "tok", "head"),
            P("section", "tok", "head"),
            P("section", None, "head"),
            P("section", "tok", "head"),
            P("section", None),
            P(),
            P(),
        ),
        out_specs=P("section", None, "tok", "head"),
        check_vma=False,
    )
```

```python
import functools

import jax
import jax.numpy as jnp
from jax import lax
from jax.experimental import pallas as pl
from jax.experimental.pallas import tpu as pltpu
from jax.sharding import PartitionSpec as P

HD = 128
GUIDE = 3.0
MESH = pl.DeviceIdType.MESH
LOG2E = 1.4426950408889634
NT = (((1,), (1,)), ((), ()))
QCHUNK = 256
PIECES = 5
K_AT = 1
Q_AT = 1
WEIGH_AT = 4
PER_STEP = 2


def kernel(
    n_sec,
    n_head,
    n_tok,
    held,
    qs,
    ks,
    vw,
    ow,
    bgate,
    tgate,
    tstep,
    out,
    held_v,
    scaled,
    w_full,
    v_full,
    q_all,
    k_all,
    g_all,
    probs,
    grad,
    o_buf,
    vgrad,
    part,
    part_in,
    own,
    pair,
    pair_in,
    held_next,
    load_sem,
    a_send,
    a_recv,
    r_send,
    r_recv,
    q_send,
    q_recv,
    k_send,
    k_recv,
    g_send,
    g_recv,
    o_send,
    o_recv,
    p_send,
    p_recv,
    c_send,
    c_recv,
):
    sec, head, z = lax.axis_index("section"), lax.axis_index("head"), lax.axis_index("tok")
    core = lax.rem(head, 2)
    width = held.shape[3]
    rows = held.shape[2]
    heads_here = width // HD
    wrows = ow.shape[1]
    piece_rows = wrows // PIECES
    hops = n_tok // 2
    half = rows // 2
    mate = head + 1 - 2 * core
    row_y = head // 2
    right, left = lax.rem(z + 1, n_tok), lax.rem(z + n_tok - 1, n_tok)
    my_head = z // 3
    owner = jnp.logical_and(lax.rem(z, 3) == core, z < 3 * heads_here)

    load_held = pltpu.make_async_copy(held.at[0], held_v, load_sem.at[0])
    load_held.start()
    load_w = pltpu.make_async_copy(
        ow.at[0], w_full.at[pl.ds(pl.multiple_of(z * wrows, 16), wrows), :], load_sem.at[1]
    )
    load_w.start()
    load_v = pltpu.make_async_copy(vw.at[0], v_full, load_sem.at[2])
    load_v.start()

    barrier = pltpu.get_barrier_semaphore()
    for step in range(1, n_tok):
        pl.semaphore_signal(
            barrier, inc=1, device_id={"tok": lax.rem(z + step, n_tok)}, device_id_type=MESH
        )
    for step in range(1, n_head):
        pl.semaphore_signal(
            barrier, inc=1, device_id={"head": lax.rem(head + step, n_head)}, device_id_type=MESH
        )
    for step in (1, n_sec - 1):
        for turn in (0, 2):
            pl.semaphore_signal(
                barrier,
                inc=1,
                device_id={
                    "section": lax.rem(sec + step, n_sec),
                    "head": lax.rem(head + turn, n_head),
                },
                device_id_type=MESH,
            )
    pl.semaphore_wait(barrier, n_tok - 1 + n_head - 1 + 4)

    def ring(direction, index, step):
        block = lax.rem(z + n_tok - step, n_tok) if direction == 0 else lax.rem(z + step, n_tok)
        start = pl.multiple_of(block * wrows + index * piece_rows, 16)
        view = w_full.at[pl.ds(start, piece_rows), :]
        return pltpu.make_async_remote_copy(
            src_ref=view,
            dst_ref=view,
            send_sem=r_send.at[direction, index, step],
            recv_sem=r_recv.at[direction, index, step],
            device_id={"tok": right if direction == 0 else left},
            device_id_type=MESH,
        )

    def reach(direction, index):
        return hops - (direction + index) % 2

    load_w.wait()
    for index in range(PIECES):
        for direction in (0, 1):
            ring(direction, index, 0).start()

    time_row = jnp.sum(
        jnp.where(
            lax.broadcasted_iota(jnp.int32, (tgate.shape[0], width), 0) == tstep[0],
            tgate[:, pl.ds(pl.multiple_of(head * width, 128), width)],
            0.0,
        ),
        axis=0,
        keepdims=True,
    )
    gate_row = bgate[:, pl.ds(pl.multiple_of(head * width, 128), width)] + time_row
    load_held.wait()
    for branch in (0, 1):
        scaled[head, branch * rows : (branch + 1) * rows, :] = (
            held_v[branch].astype(jnp.float32) * gate_row
        ).astype(jnp.bfloat16)

    def to_mate(step):
        return pltpu.make_async_remote_copy(
            src_ref=scaled.at[head],
            dst_ref=scaled.at[head],
            send_sem=a_send.at[step - 1],
            recv_sem=a_recv.at[step - 1],
            device_id={"head": lax.rem(head + step, n_head)},
            device_id_type=MESH,
        )

    for step in range(1, n_head):
        to_mate(step).start()

    def hand_down(source, target, send_sem, recv_sem, head_index):
        return pltpu.make_async_remote_copy(
            src_ref=source,
            dst_ref=target,
            send_sem=send_sem,
            recv_sem=recv_sem,
            device_id={"section": lax.rem(sec + n_sec - 1, n_sec), "head": head_index},
            device_id_type=MESH,
        )

    def held_copy():
        return hand_down(held_v, held_next, c_send.at[0], c_recv.at[0], head)

    sends_down = sec > 0
    takes_down = sec < n_sec - 1
    pl.when(sends_down)(lambda: held_copy().start())

    def to_owner(source, target_ref, send_sem, recv_sem, index):
        owner_z = 3 * index + core

        @pl.when(owner_z == z)
        def _():
            pltpu.make_async_copy(source, target_ref.at[z], recv_sem).start()

        @pl.when(owner_z != z)
        def _():
            pltpu.make_async_remote_copy(
                src_ref=source,
                dst_ref=target_ref.at[z],
                send_sem=send_sem.at[index],
                recv_sem=recv_sem,
                device_id={"tok": owner_z},
                device_id_type=MESH,
            ).start()

    def wait_to_owner(source, target_ref, send_sem, recv_sem, index):
        owner_z = 3 * index + core

        @pl.when(owner_z != z)
        def _():
            pltpu.make_async_remote_copy(
                src_ref=source,
                dst_ref=target_ref.at[z],
                send_sem=send_sem.at[index],
                recv_sem=recv_sem,
                device_id={"tok": owner_z},
                device_id_type=MESH,
            ).wait_send()

    def head_cols(index):
        return slice(index * HD, (index + 1) * HD)

    def key_part(side, index):
        return ks.at[0, side * half : (side + 1) * half, head_cols(index)]

    def send_keys():
        for index in range(heads_here):
            for side in (0, 1):
                to_owner(key_part(side, index), k_all.at[side], k_send.at[side], k_recv, index)

    def send_queries():
        for index in range(heads_here):
            to_owner(qs.at[0, :, head_cols(index)], q_all, q_send, q_recv.at[z], index)

    chunks = n_tok * rows // QCHUNK
    per_chunk = QCHUNK // rows

    def weigh(chunk):
        query = q_all[pl.ds(chunk * per_chunk, per_chunk)].reshape(QCHUNK, HD)
        key = k_all[...].reshape(n_tok * rows, HD)
        raw = lax.dot_general(key, query, NT, preferred_element_type=jnp.float32) * (
            HD ** (-0.5) * LOG2E
        )
        top = jnp.max(raw, axis=0, keepdims=True)
        grown = jnp.exp2(raw - top)
        total = jnp.sum(grown, axis=0, keepdims=True)
        cols = pl.ds(pl.multiple_of(chunk * QCHUNK, QCHUNK), QCHUNK)
        probs[:, cols] = (grown * (1.0 / total)).astype(jnp.bfloat16)

    def advance(step):
        for index in range(PIECES):
            for direction in (0, 1):
                count = reach(direction, index)

                @pl.when(step <= count)
                def _():
                    ring(direction, index, step - 1).wait_recv()

                @pl.when(step < count)
                def _():
                    ring(direction, index, step).start()

    def weigh_turn(turn):
        @pl.when(turn == 0)
        def _():
            pltpu.make_async_copy(k_all, k_all, k_recv).wait()

        shift = (turn + 1) // 2 * (2 * lax.rem(turn, 2) - 1)
        chunk = lax.rem(z // per_chunk + shift + chunks, chunks)
        for place in range(per_chunk):
            source = chunk * per_chunk + place
            view = q_all.at[source]
            pltpu.make_async_copy(view, view, q_recv.at[source]).wait()
        weigh(chunk)

    weighed = min(chunks, PER_STEP * (hops - WEIGH_AT))

    @pl.loop(1, hops + 1)
    def _(step):
        @pl.when(step == K_AT)
        def _():
            send_keys()

        @pl.when(step == Q_AT)
        def _():
            send_queries()

        advance(step)

        @pl.when(jnp.logical_and(owner, jnp.logical_and(step >= WEIGH_AT, step < hops)))
        def _():
            first = (step - WEIGH_AT) * PER_STEP

            @pl.loop(0, PER_STEP)
            def _(turn):
                pl.when(first + turn < weighed)(lambda: weigh_turn(first + turn))

    for step in range(1, n_head):
        to_mate(step).wait_recv()

    for low in range(0, width, 2 * HD):
        high = min(low + 2 * HD, width)
        total = None
        for part_head in range(n_head):
            term = jnp.dot(
                scaled[part_head],
                w_full[part_head * width : (part_head + 1) * width, low:high],
                preferred_element_type=jnp.float32,
            )
            total = term if total is None else total + term
        for branch in (0, 1):
            grad[branch, :, low:high] = total[branch * rows : (branch + 1) * rows].astype(jnp.bfloat16)
        for index in range(low // HD, high // HD):
            to_owner(grad.at[0, :, head_cols(index)], g_all, g_send, g_recv, index)

    load_v.wait()

    def exchange(branch, side):
        return pltpu.make_async_remote_copy(
            src_ref=part.at[branch, side],
            dst_ref=part_in.at[branch, side],
            send_sem=p_send.at[branch, side],
            recv_sem=p_recv.at[branch, side],
            device_id={"head": mate},
            device_id_type=MESH,
        )

    def pair_down(branch, side, y):
        slot = (branch * 2 + side) * 2
        return hand_down(
            pair.at[branch, side, y],
            pair_in.at[branch, side, row_y],
            c_send.at[1 + slot + y],
            c_recv.at[1 + slot + row_y],
            2 * y + core,
        )

    def project(branch, side, value):
        def back(target):
            weight = v_full[pl.ds(pl.multiple_of(target * width, 128), width), :]
            return lax.dot_general(value, weight, NT, preferred_element_type=jnp.float32)

        for y in range(n_head // 2):
            part[branch, side, y] = back(2 * y + 1 - core).astype(jnp.bfloat16)
        exchange(branch, side).start()
        for y in range(n_head // 2):
            own[y] = back(2 * y + core)
        exchange(branch, side).wait_recv()
        for y in range(n_head // 2):
            total = own[y] + part_in[branch, side, y].astype(jnp.float32)
            pair[branch, side, y] = total.astype(jnp.bfloat16)
            pl.when(sends_down)(lambda: pair_down(branch, side, y).start())

    def collect(branch, side):
        @pl.when(takes_down)
        def _():
            for y in range(n_head // 2):
                slot = (branch * 2 + side) * 2 + y
                view = pair_in.at[branch, side, y]
                pltpu.make_async_copy(view, view, c_recv.at[1 + slot]).wait()
            span = slice(side * half, (side + 1) * half)
            total = held_next[branch, span, :].astype(jnp.float32)
            for y in range(n_head // 2):
                total = total + pair_in[branch, side, y].astype(jnp.float32)
            out[branch, span, :] = total.astype(jnp.bfloat16)

    own_cols = pl.ds(pl.multiple_of(my_head * HD, HD), HD)

    def back_to(side, block):
        return pltpu.make_async_remote_copy(
            src_ref=o_buf.at[side, block],
            dst_ref=vgrad.at[side, :, own_cols],
            send_sem=o_send.at[side, block],
            recv_sem=o_recv.at[side],
            device_id={"tok": block},
            device_id_type=MESH,
        )

    for side in (0, 1):
        project(1, side, grad[1, side * half : (side + 1) * half, :])

    together = 2 * rows // half

    @pl.when(owner)
    def _():
        @pl.loop(weighed, chunks)
        def _(turn):
            weigh_turn(turn)

        pltpu.make_async_copy(g_all, g_all, g_recv).wait()
        groups = n_tok // together

        for side in (0, 1):

            @pl.loop(0, groups)
            def _(turn):
                base = lax.rem(z // together + groups // 2 + turn, groups) * together
                start = pl.multiple_of((side * n_tok + base) * half, together * half)
                several = jnp.dot(
                    probs[pl.ds(start, together * half), :],
                    g_all[...].reshape(n_tok * rows, HD),
                    preferred_element_type=jnp.float32,
                ).astype(jnp.bfloat16)
                for place in range(together):
                    block = base + place
                    o_buf[side, block] = several[place * half : (place + 1) * half]

                    @pl.when(block == z)
                    def _():
                        pltpu.make_async_copy(
                            o_buf.at[side, block], vgrad.at[side, :, own_cols], o_recv.at[side]
                        ).start()

                    @pl.when(block != z)
                    def _():
                        back_to(side, block).start()

    @pl.when(takes_down)
    def _():
        pltpu.make_async_copy(held_next, held_next, c_recv.at[0]).wait()

    @pl.when(jnp.logical_not(takes_down))
    def _():
        out[...] = jnp.zeros_like(out)

    for side in (0, 1):
        collect(1, side)
    for side in (0, 1):
        pltpu.make_async_copy(vgrad.at[side], vgrad.at[side], o_recv.at[side]).wait()
        project(0, side, vgrad[side])
    for side in (0, 1):
        collect(0, side)

    for index in range(heads_here):
        for side in (0, 1):
            wait_to_owner(key_part(side, index), k_all.at[side], k_send.at[side], k_recv, index)
        wait_to_owner(qs.at[0, :, head_cols(index)], q_all, q_send, q_recv.at[z], index)
        wait_to_owner(grad.at[0, :, head_cols(index)], g_all, g_send, g_recv, index)

    for index in range(PIECES):
        for direction in (0, 1):

            @pl.loop(0, reach(direction, index))
            def _(step):
                ring(direction, index, step).wait_send()

    @pl.when(owner)
    def _():
        for side in (0, 1):

            @pl.loop(0, n_tok)
            def _(block):
                @pl.when(block != z)
                def _():
                    back_to(side, block).wait_send()

    for step in range(1, n_head):
        to_mate(step).wait_send()
    for branch in (0, 1):
        for side in (0, 1):
            exchange(branch, side).wait_send()

    @pl.when(sends_down)
    def _():
        held_copy().wait_send()
        for branch in (0, 1):
            for side in (0, 1):
                for y in range(n_head // 2):
                    pair_down(branch, side, y).wait_send()


def shards(
    sizes,
    held_cotangents,
    entering_adjoint,
    saved_queries,
    saved_keys,
    value_weight,
    out_weight,
    block_gate,
    time_gate,
    timestep,
):
    n_sec, n_head, n_tok = sizes
    _, branches, rows, width = held_cotangents.shape
    heads_here = width // HD
    model = block_gate.shape[1]
    tokens = n_tok * rows
    bf16 = jnp.bfloat16
    dma = pltpu.SemaphoreType.DMA
    anywhere = pl.BlockSpec(memory_space=pl.ANY)
    vmem = pl.BlockSpec(memory_space=pltpu.VMEM)
    passed_on = pl.pallas_call(
        functools.partial(kernel, n_sec, n_head, n_tok),
        out_shape=jax.ShapeDtypeStruct((branches, rows, width), bf16),
        in_specs=[anywhere] * 5 + [vmem, vmem, pl.BlockSpec(memory_space=pltpu.SMEM)],
        out_specs=vmem,
        scratch_shapes=[
            pltpu.VMEM((branches, rows, width), bf16),
            pltpu.VMEM((n_head, branches * rows, width), bf16),
            pltpu.VMEM((model, width), bf16),
            pltpu.VMEM((model, width), bf16),
            pltpu.VMEM((n_tok, rows, HD), bf16),
            pltpu.VMEM((2, n_tok, rows // 2, HD), bf16),
            pltpu.VMEM((n_tok, rows, HD), bf16),
            pltpu.VMEM((tokens, tokens), bf16),
            pltpu.VMEM((branches, rows, width), bf16),
            pltpu.VMEM((2, n_tok, rows // 2, HD), bf16),
            pltpu.VMEM((2, rows // 2, width), bf16),
            pltpu.VMEM((branches, 2, n_head // 2, rows // 2, width), bf16),
            pltpu.VMEM((branches, 2, n_head // 2, rows // 2, width), bf16),
            pltpu.VMEM((n_head // 2, rows // 2, width), jnp.float32),
            pltpu.VMEM((branches, 2, n_head // 2, rows // 2, width), bf16),
            pltpu.VMEM((branches, 2, n_head // 2, rows // 2, width), bf16),
            pltpu.VMEM((branches, rows, width), bf16),
            dma((3,)),
            dma((n_head - 1,)),
            dma((n_head - 1,)),
            dma((2, PIECES, n_tok // 2)),
            dma((2, PIECES, n_tok // 2)),
            dma((heads_here,)),
            dma((n_tok,)),
            dma((2, heads_here)),
            dma,
            dma((heads_here,)),
            dma,
            dma((2, n_tok)),
            dma((2,)),
            dma((branches, 2)),
            dma((branches, 2)),
            dma((9,)),
            dma((9,)),
        ],
        compiler_params=pltpu.CompilerParams(
            collective_id=0, has_side_effects=True, vmem_limit_bytes=56 * 1024 * 1024
        ),
        name="tick",
    )(
        held_cotangents,
        saved_queries,
        saved_keys,
        value_weight,
        out_weight,
        block_gate,
        time_gate,
        timestep,
    )
    entering_full = entering_adjoint.astype(jnp.float32)
    fresh_rows = jnp.stack([(1.0 + GUIDE) * entering_full, -GUIDE * entering_full]).astype(bf16)
    is_last = lax.axis_index("section") == n_sec - 1
    return jnp.where(is_last, fresh_rows, passed_on)[None]


def solution(mesh):
    sizes = (mesh.shape["section"], mesh.shape["head"], mesh.shape["tok"])
    return jax.shard_map(
        functools.partial(shards, sizes),
        mesh=mesh,
        in_specs=(
            P("section", None, "tok", "head"),
            P("tok", "head"),
            P("section", "tok", "head"),
            P("section", "tok", "head"),
            P("section", None, "head"),
            P("section", "tok", "head"),
            P("section", None),
            P(),
            P(),
        ),
        out_specs=P("section", None, "tok", "head"),
        check_vma=False,
    )
```

```python
import functools

import jax
import jax.numpy as jnp
from jax import lax
from jax.experimental import pallas as pl
from jax.experimental.pallas import tpu as pltpu
from jax.sharding import PartitionSpec as P

HD = 128
GUIDE = 3.0
MESH = pl.DeviceIdType.MESH
LOG2E = 1.4426950408889634
NT = (((1,), (1,)), ((), ()))
QCHUNK = 256
PIECES = 5
K_AT = 1
Q_AT = 1
WEIGH_AT = 4
PER_STEP = 2


def kernel(
    n_sec,
    n_head,
    n_tok,
    held,
    qs,
    ks,
    vw,
    ow,
    bgate,
    tgate,
    tstep,
    out,
    held_v,
    scaled,
    w_full,
    v_full,
    q_all,
    k_all,
    g_all,
    probs,
    grad,
    o_buf,
    vgrad,
    part,
    part_in,
    own,
    pair,
    pair_in,
    held_next,
    load_sem,
    a_send,
    a_recv,
    r_send,
    r_recv,
    q_send,
    q_recv,
    k_send,
    k_recv,
    g_send,
    g_recv,
    o_send,
    o_recv,
    p_send,
    p_recv,
    c_send,
    c_recv,
):
    sec, head, z = lax.axis_index("section"), lax.axis_index("head"), lax.axis_index("tok")
    core = lax.rem(head, 2)
    width = held.shape[3]
    rows = held.shape[2]
    heads_here = width // HD
    wrows = ow.shape[1]
    piece_rows = wrows // PIECES
    hops = n_tok // 2
    half = rows // 2
    mate = head + 1 - 2 * core
    row_y = head // 2
    right, left = lax.rem(z + 1, n_tok), lax.rem(z + n_tok - 1, n_tok)
    my_head = z // 3
    owner = jnp.logical_and(lax.rem(z, 3) == core, z < 3 * heads_here)

    load_held = pltpu.make_async_copy(held.at[0], held_v, load_sem.at[0])
    load_held.start()
    load_w = pltpu.make_async_copy(
        ow.at[0], w_full.at[pl.ds(pl.multiple_of(z * wrows, 16), wrows), :], load_sem.at[1]
    )
    load_w.start()
    load_v = pltpu.make_async_copy(vw.at[0], v_full, load_sem.at[2])
    load_v.start()

    barrier = pltpu.get_barrier_semaphore()
    for step in range(1, n_tok):
        pl.semaphore_signal(
            barrier, inc=1, device_id={"tok": lax.rem(z + step, n_tok)}, device_id_type=MESH
        )
    for step in range(1, n_head):
        pl.semaphore_signal(
            barrier, inc=1, device_id={"head": lax.rem(head + step, n_head)}, device_id_type=MESH
        )
    for step in (1, n_sec - 1):
        for turn in (0, 2):
            pl.semaphore_signal(
                barrier,
                inc=1,
                device_id={
                    "section": lax.rem(sec + step, n_sec),
                    "head": lax.rem(head + turn, n_head),
                },
                device_id_type=MESH,
            )
    pl.semaphore_wait(barrier, n_tok - 1 + n_head - 1 + 4)

    def ring(direction, index, step):
        block = lax.rem(z + n_tok - step, n_tok) if direction == 0 else lax.rem(z + step, n_tok)
        start = pl.multiple_of(block * wrows + index * piece_rows, 16)
        view = w_full.at[pl.ds(start, piece_rows), :]
        return pltpu.make_async_remote_copy(
            src_ref=view,
            dst_ref=view,
            send_sem=r_send.at[direction, index, step],
            recv_sem=r_recv.at[direction, index, step],
            device_id={"tok": right if direction == 0 else left},
            device_id_type=MESH,
        )

    def reach(direction, index):
        return hops - (direction + index) % 2

    load_w.wait()
    for index in range(PIECES):
        for direction in (0, 1):
            ring(direction, index, 0).start()

    time_row = jnp.sum(
        jnp.where(
            lax.broadcasted_iota(jnp.int32, (tgate.shape[0], width), 0) == tstep[0],
            tgate[:, pl.ds(pl.multiple_of(head * width, 128), width)],
            0.0,
        ),
        axis=0,
        keepdims=True,
    )
    gate_row = bgate[:, pl.ds(pl.multiple_of(head * width, 128), width)] + time_row
    load_held.wait()
    for branch in (0, 1):
        scaled[head, branch * rows : (branch + 1) * rows, :] = (
            held_v[branch].astype(jnp.float32) * gate_row
        ).astype(jnp.bfloat16)

    def to_mate(step):
        return pltpu.make_async_remote_copy(
            src_ref=scaled.at[head],
            dst_ref=scaled.at[head],
            send_sem=a_send.at[step - 1],
            recv_sem=a_recv.at[step - 1],
            device_id={"head": lax.rem(head + step, n_head)},
            device_id_type=MESH,
        )

    for step in range(1, n_head):
        to_mate(step).start()

    def hand_down(source, target, send_sem, recv_sem, head_index):
        return pltpu.make_async_remote_copy(
            src_ref=source,
            dst_ref=target,
            send_sem=send_sem,
            recv_sem=recv_sem,
            device_id={"section": lax.rem(sec + n_sec - 1, n_sec), "head": head_index},
            device_id_type=MESH,
        )

    def held_copy():
        return hand_down(held_v, held_next, c_send.at[0], c_recv.at[0], head)

    sends_down = sec > 0
    takes_down = sec < n_sec - 1
    pl.when(sends_down)(lambda: held_copy().start())

    def to_owner(source, target_ref, send_sem, recv_sem, index):
        owner_z = 3 * index + core

        @pl.when(owner_z == z)
        def _():
            pltpu.make_async_copy(source, target_ref.at[z], recv_sem).start()

        @pl.when(owner_z != z)
        def _():
            pltpu.make_async_remote_copy(
                src_ref=source,
                dst_ref=target_ref.at[z],
                send_sem=send_sem.at[index],
                recv_sem=recv_sem,
                device_id={"tok": owner_z},
                device_id_type=MESH,
            ).start()

    def wait_to_owner(source, target_ref, send_sem, recv_sem, index):
        owner_z = 3 * index + core

        @pl.when(owner_z != z)
        def _():
            pltpu.make_async_remote_copy(
                src_ref=source,
                dst_ref=target_ref.at[z],
                send_sem=send_sem.at[index],
                recv_sem=recv_sem,
                device_id={"tok": owner_z},
                device_id_type=MESH,
            ).wait_send()

    def head_cols(index):
        return pl.ds(pl.multiple_of(index * HD, HD), HD)

    turns = (2, 3, 1, 4, 0)

    def spread(turn):
        return lax.rem(z // 3 + turn, heads_here)

    def key_part(side, index):
        return ks.at[0, side * half : (side + 1) * half, head_cols(index)]

    def send_keys():
        for index in map(spread, turns):
            for side in (0, 1):
                to_owner(key_part(side, index), k_all.at[side], k_send.at[side], k_recv, index)

    def send_queries():
        for index in map(spread, turns):
            to_owner(qs.at[0, :, head_cols(index)], q_all, q_send, q_recv.at[z], index)

    chunks = n_tok * rows // QCHUNK
    per_chunk = QCHUNK // rows

    def weigh(chunk):
        query = q_all[pl.ds(chunk * per_chunk, per_chunk)].reshape(QCHUNK, HD)
        key = k_all[...].reshape(n_tok * rows, HD)
        raw = lax.dot_general(key, query, NT, preferred_element_type=jnp.float32) * (
            HD ** (-0.5) * LOG2E
        )
        top = jnp.max(raw, axis=0, keepdims=True)
        grown = jnp.exp2(raw - top)
        total = jnp.sum(grown, axis=0, keepdims=True)
        cols = pl.ds(pl.multiple_of(chunk * QCHUNK, QCHUNK), QCHUNK)
        probs[:, cols] = (grown * (1.0 / total)).astype(jnp.bfloat16)

    def advance(step):
        for index in range(PIECES):
            for direction in (0, 1):
                count = reach(direction, index)

                @pl.when(step <= count)
                def _():
                    ring(direction, index, step - 1).wait_recv()

                @pl.when(step < count)
                def _():
                    ring(direction, index, step).start()

    def weigh_turn(turn):
        @pl.when(turn == 0)
        def _():
            pltpu.make_async_copy(k_all, k_all, k_recv).wait()

        shift = (turn + 1) // 2 * (2 * lax.rem(turn, 2) - 1)
        chunk = lax.rem(z // per_chunk + shift + chunks, chunks)
        for place in range(per_chunk):
            source = chunk * per_chunk + place
            view = q_all.at[source]
            pltpu.make_async_copy(view, view, q_recv.at[source]).wait()
        weigh(chunk)

    weighed = min(chunks, PER_STEP * (hops - WEIGH_AT))

    @pl.loop(1, hops + 1)
    def _(step):
        @pl.when(step == K_AT)
        def _():
            send_keys()

        @pl.when(step == Q_AT)
        def _():
            send_queries()

        advance(step)

        @pl.when(jnp.logical_and(owner, jnp.logical_and(step >= WEIGH_AT, step < hops)))
        def _():
            first = (step - WEIGH_AT) * PER_STEP

            @pl.loop(0, PER_STEP)
            def _(turn):
                pl.when(first + turn < weighed)(lambda: weigh_turn(first + turn))

    for step in range(1, n_head):
        to_mate(step).wait_recv()

    for index in map(spread, turns):
        total = None
        for source in range(n_head):
            term = jnp.dot(
                scaled[source],
                w_full[source * width : (source + 1) * width, head_cols(index)],
                preferred_element_type=jnp.float32,
            )
            total = term if total is None else total + term
        for branch in (0, 1):
            grad[branch, :, head_cols(index)] = total[branch * rows : (branch + 1) * rows].astype(
                jnp.bfloat16
            )
        to_owner(grad.at[0, :, head_cols(index)], g_all, g_send, g_recv, index)

    load_v.wait()

    def exchange(branch, side):
        return pltpu.make_async_remote_copy(
            src_ref=part.at[branch, side],
            dst_ref=part_in.at[branch, side],
            send_sem=p_send.at[branch, side],
            recv_sem=p_recv.at[branch, side],
            device_id={"head": mate},
            device_id_type=MESH,
        )

    def pair_down(branch, side, y):
        slot = (branch * 2 + side) * 2
        return hand_down(
            pair.at[branch, side, y],
            pair_in.at[branch, side, row_y],
            c_send.at[1 + slot + y],
            c_recv.at[1 + slot + row_y],
            2 * y + core,
        )

    def project(branch, side, value):
        def back(target):
            weight = v_full[pl.ds(pl.multiple_of(target * width, 128), width), :]
            return lax.dot_general(value, weight, NT, preferred_element_type=jnp.float32)

        for y in range(n_head // 2):
            part[branch, side, y] = back(2 * y + 1 - core).astype(jnp.bfloat16)
        exchange(branch, side).start()
        for y in range(n_head // 2):
            own[y] = back(2 * y + core)
        exchange(branch, side).wait_recv()
        for y in range(n_head // 2):
            total = own[y] + part_in[branch, side, y].astype(jnp.float32)
            pair[branch, side, y] = total.astype(jnp.bfloat16)
            pl.when(sends_down)(lambda: pair_down(branch, side, y).start())

    def collect(branch, side):
        @pl.when(takes_down)
        def _():
            for y in range(n_head // 2):
                slot = (branch * 2 + side) * 2 + y
                view = pair_in.at[branch, side, y]
                pltpu.make_async_copy(view, view, c_recv.at[1 + slot]).wait()
            span = slice(side * half, (side + 1) * half)
            total = held_next[branch, span, :].astype(jnp.float32)
            for y in range(n_head // 2):
                total = total + pair_in[branch, side, y].astype(jnp.float32)
            out[branch, span, :] = total.astype(jnp.bfloat16)

    own_cols = pl.ds(pl.multiple_of(my_head * HD, HD), HD)

    def back_to(side, block):
        return pltpu.make_async_remote_copy(
            src_ref=o_buf.at[side, block],
            dst_ref=vgrad.at[side, :, own_cols],
            send_sem=o_send.at[side, block],
            recv_sem=o_recv.at[side],
            device_id={"tok": block},
            device_id_type=MESH,
        )

    for side in (0, 1):
        project(1, side, grad[1, side * half : (side + 1) * half, :])

    together = 2 * rows // half

    @pl.when(owner)
    def _():
        @pl.loop(weighed, chunks)
        def _(turn):
            weigh_turn(turn)

        pltpu.make_async_copy(g_all, g_all, g_recv).wait()
        groups = n_tok // together

        for side in (0, 1):

            @pl.loop(0, groups)
            def _(turn):
                base = lax.rem(z // together + groups // 2 + turn, groups) * together
                start = pl.multiple_of((side * n_tok + base) * half, together * half)
                several = jnp.dot(
                    probs[pl.ds(start, together * half), :],
                    g_all[...].reshape(n_tok * rows, HD),
                    preferred_element_type=jnp.float32,
                ).astype(jnp.bfloat16)
                for place in range(together):
                    block = base + place
                    o_buf[side, block] = several[place * half : (place + 1) * half]

                    @pl.when(block == z)
                    def _():
                        pltpu.make_async_copy(
                            o_buf.at[side, block], vgrad.at[side, :, own_cols], o_recv.at[side]
                        ).start()

                    @pl.when(block != z)
                    def _():
                        back_to(side, block).start()

    @pl.when(takes_down)
    def _():
        pltpu.make_async_copy(held_next, held_next, c_recv.at[0]).wait()

    @pl.when(jnp.logical_not(takes_down))
    def _():
        out[...] = jnp.zeros_like(out)

    for side in (0, 1):
        collect(1, side)
    for side in (0, 1):
        pltpu.make_async_copy(vgrad.at[side], vgrad.at[side], o_recv.at[side]).wait()
        project(0, side, vgrad[side])
    for side in (0, 1):
        collect(0, side)

    for index in range(heads_here):
        for side in (0, 1):
            wait_to_owner(key_part(side, index), k_all.at[side], k_send.at[side], k_recv, index)
        wait_to_owner(qs.at[0, :, head_cols(index)], q_all, q_send, q_recv.at[z], index)
        wait_to_owner(grad.at[0, :, head_cols(index)], g_all, g_send, g_recv, index)

    for index in range(PIECES):
        for direction in (0, 1):

            @pl.loop(0, reach(direction, index))
            def _(step):
                ring(direction, index, step).wait_send()

    @pl.when(owner)
    def _():
        for side in (0, 1):

            @pl.loop(0, n_tok)
            def _(block):
                @pl.when(block != z)
                def _():
                    back_to(side, block).wait_send()

    for step in range(1, n_head):
        to_mate(step).wait_send()
    for branch in (0, 1):
        for side in (0, 1):
            exchange(branch, side).wait_send()

    @pl.when(sends_down)
    def _():
        held_copy().wait_send()
        for branch in (0, 1):
            for side in (0, 1):
                for y in range(n_head // 2):
                    pair_down(branch, side, y).wait_send()


def shards(
    sizes,
    held_cotangents,
    entering_adjoint,
    saved_queries,
    saved_keys,
    value_weight,
    out_weight,
    block_gate,
    time_gate,
    timestep,
):
    n_sec, n_head, n_tok = sizes
    _, branches, rows, width = held_cotangents.shape
    heads_here = width // HD
    model = block_gate.shape[1]
    tokens = n_tok * rows
    bf16 = jnp.bfloat16
    dma = pltpu.SemaphoreType.DMA
    anywhere = pl.BlockSpec(memory_space=pl.ANY)
    vmem = pl.BlockSpec(memory_space=pltpu.VMEM)
    passed_on = pl.pallas_call(
        functools.partial(kernel, n_sec, n_head, n_tok),
        out_shape=jax.ShapeDtypeStruct((branches, rows, width), bf16),
        in_specs=[anywhere] * 5 + [vmem, vmem, pl.BlockSpec(memory_space=pltpu.SMEM)],
        out_specs=vmem,
        scratch_shapes=[
            pltpu.VMEM((branches, rows, width), bf16),
            pltpu.VMEM((n_head, branches * rows, width), bf16),
            pltpu.VMEM((model, width), bf16),
            pltpu.VMEM((model, width), bf16),
            pltpu.VMEM((n_tok, rows, HD), bf16),
            pltpu.VMEM((2, n_tok, rows // 2, HD), bf16),
            pltpu.VMEM((n_tok, rows, HD), bf16),
            pltpu.VMEM((tokens, tokens), bf16),
            pltpu.VMEM((branches, rows, width), bf16),
            pltpu.VMEM((2, n_tok, rows // 2, HD), bf16),
            pltpu.VMEM((2, rows // 2, width), bf16),
            pltpu.VMEM((branches, 2, n_head // 2, rows // 2, width), bf16),
            pltpu.VMEM((branches, 2, n_head // 2, rows // 2, width), bf16),
            pltpu.VMEM((n_head // 2, rows // 2, width), jnp.float32),
            pltpu.VMEM((branches, 2, n_head // 2, rows // 2, width), bf16),
            pltpu.VMEM((branches, 2, n_head // 2, rows // 2, width), bf16),
            pltpu.VMEM((branches, rows, width), bf16),
            dma((3,)),
            dma((n_head - 1,)),
            dma((n_head - 1,)),
            dma((2, PIECES, n_tok // 2)),
            dma((2, PIECES, n_tok // 2)),
            dma((heads_here,)),
            dma((n_tok,)),
            dma((2, heads_here)),
            dma,
            dma((heads_here,)),
            dma,
            dma((2, n_tok)),
            dma((2,)),
            dma((branches, 2)),
            dma((branches, 2)),
            dma((9,)),
            dma((9,)),
        ],
        compiler_params=pltpu.CompilerParams(
            collective_id=0, has_side_effects=True, vmem_limit_bytes=56 * 1024 * 1024
        ),
        name="tick",
    )(
        held_cotangents,
        saved_queries,
        saved_keys,
        value_weight,
        out_weight,
        block_gate,
        time_gate,
        timestep,
    )
    entering_full = entering_adjoint.astype(jnp.float32)
    fresh_rows = jnp.stack([(1.0 + GUIDE) * entering_full, -GUIDE * entering_full]).astype(bf16)
    is_last = lax.axis_index("section") == n_sec - 1
    return jnp.where(is_last, fresh_rows, passed_on)[None]


def solution(mesh):
    sizes = (mesh.shape["section"], mesh.shape["head"], mesh.shape["tok"])
    return jax.shard_map(
        functools.partial(shards, sizes),
        mesh=mesh,
        in_specs=(
            P("section", None, "tok", "head"),
            P("tok", "head"),
            P("section", "tok", "head"),
            P("section", "tok", "head"),
            P("section", None, "head"),
            P("section", "tok", "head"),
            P("section", None),
            P(),
            P(),
        ),
        out_specs=P("section", None, "tok", "head"),
        check_vma=False,
    )
```

```python
import functools

import jax
import jax.numpy as jnp
from jax import lax
from jax.experimental import pallas as pl
from jax.experimental.pallas import tpu as pltpu
from jax.sharding import PartitionSpec as P

HD = 128
GUIDE = 3.0
MESH = pl.DeviceIdType.MESH
LOG2E = 1.4426950408889634
NT = (((1,), (1,)), ((), ()))
QCHUNK = 256
PIECES = 5
K_AT = 2
Q_AT = 2
WEIGH_AT = 4
PER_STEP = 2


def kernel(
    n_sec,
    n_head,
    n_tok,
    held,
    qs,
    ks,
    vw,
    ow,
    bgate,
    tgate,
    tstep,
    out,
    held_v,
    scaled,
    w_full,
    v_full,
    q_all,
    k_all,
    g_all,
    probs,
    grad,
    o_buf,
    vgrad,
    part,
    part_in,
    own,
    pair,
    pair_in,
    held_next,
    load_sem,
    a_send,
    a_recv,
    r_send,
    r_recv,
    q_send,
    q_recv,
    k_send,
    k_recv,
    g_send,
    g_recv,
    o_send,
    o_recv,
    p_send,
    p_recv,
    c_send,
    c_recv,
):
    sec, head, z = lax.axis_index("section"), lax.axis_index("head"), lax.axis_index("tok")
    core = lax.rem(head, 2)
    width = held.shape[3]
    rows = held.shape[2]
    heads_here = width // HD
    wrows = ow.shape[1]
    piece_rows = wrows // PIECES
    hops = n_tok // 2
    half = rows // 2
    mate = head + 1 - 2 * core
    row_y = head // 2
    right, left = lax.rem(z + 1, n_tok), lax.rem(z + n_tok - 1, n_tok)
    my_head = z // 3
    owner = jnp.logical_and(lax.rem(z, 3) == core, z < 3 * heads_here)

    load_held = pltpu.make_async_copy(held.at[0], held_v, load_sem.at[0])
    load_held.start()
    load_w = pltpu.make_async_copy(
        ow.at[0], w_full.at[pl.ds(pl.multiple_of(z * wrows, 16), wrows), :], load_sem.at[1]
    )
    load_w.start()
    load_v = pltpu.make_async_copy(vw.at[0], v_full, load_sem.at[2])
    load_v.start()

    barrier = pltpu.get_barrier_semaphore()
    for step in range(1, n_tok):
        pl.semaphore_signal(
            barrier, inc=1, device_id={"tok": lax.rem(z + step, n_tok)}, device_id_type=MESH
        )
    for step in range(1, n_head):
        pl.semaphore_signal(
            barrier, inc=1, device_id={"head": lax.rem(head + step, n_head)}, device_id_type=MESH
        )
    for step in (1, n_sec - 1):
        for turn in (0, 2):
            pl.semaphore_signal(
                barrier,
                inc=1,
                device_id={
                    "section": lax.rem(sec + step, n_sec),
                    "head": lax.rem(head + turn, n_head),
                },
                device_id_type=MESH,
            )
    pl.semaphore_wait(barrier, n_tok - 1 + n_head - 1 + 4)

    def ring(direction, index, step):
        block = lax.rem(z + n_tok - step, n_tok) if direction == 0 else lax.rem(z + step, n_tok)
        start = pl.multiple_of(block * wrows + index * piece_rows, 16)
        view = w_full.at[pl.ds(start, piece_rows), :]
        return pltpu.make_async_remote_copy(
            src_ref=view,
            dst_ref=view,
            send_sem=r_send.at[direction, index, step],
            recv_sem=r_recv.at[direction, index, step],
            device_id={"tok": right if direction == 0 else left},
            device_id_type=MESH,
        )

    def reach(direction, index):
        return hops - (direction + index) % 2

    load_w.wait()
    for index in range(PIECES):
        for direction in (0, 1):
            ring(direction, index, 0).start()

    time_row = jnp.sum(
        jnp.where(
            lax.broadcasted_iota(jnp.int32, (tgate.shape[0], width), 0) == tstep[0],
            tgate[:, pl.ds(pl.multiple_of(head * width, 128), width)],
            0.0,
        ),
        axis=0,
        keepdims=True,
    )
    gate_row = bgate[:, pl.ds(pl.multiple_of(head * width, 128), width)] + time_row
    load_held.wait()
    for branch in (0, 1):
        scaled[head, branch * rows : (branch + 1) * rows, :] = (
            held_v[branch].astype(jnp.float32) * gate_row
        ).astype(jnp.bfloat16)

    def to_mate(step):
        return pltpu.make_async_remote_copy(
            src_ref=scaled.at[head],
            dst_ref=scaled.at[head],
            send_sem=a_send.at[step - 1],
            recv_sem=a_recv.at[step - 1],
            device_id={"head": lax.rem(head + step, n_head)},
            device_id_type=MESH,
        )

    for step in range(1, n_head):
        to_mate(step).start()

    def hand_down(source, target, send_sem, recv_sem, head_index):
        return pltpu.make_async_remote_copy(
            src_ref=source,
            dst_ref=target,
            send_sem=send_sem,
            recv_sem=recv_sem,
            device_id={"section": lax.rem(sec + n_sec - 1, n_sec), "head": head_index},
            device_id_type=MESH,
        )

    def held_copy():
        return hand_down(held_v, held_next, c_send.at[0], c_recv.at[0], head)

    sends_down = sec > 0
    takes_down = sec < n_sec - 1
    pl.when(sends_down)(lambda: held_copy().start())

    def to_owner(source, target_ref, send_sem, recv_sem, index):
        owner_z = 3 * index + core

        @pl.when(owner_z == z)
        def _():
            pltpu.make_async_copy(source, target_ref.at[z], recv_sem).start()

        @pl.when(owner_z != z)
        def _():
            pltpu.make_async_remote_copy(
                src_ref=source,
                dst_ref=target_ref.at[z],
                send_sem=send_sem.at[index],
                recv_sem=recv_sem,
                device_id={"tok": owner_z},
                device_id_type=MESH,
            ).start()

    def wait_to_owner(source, target_ref, send_sem, recv_sem, index):
        owner_z = 3 * index + core

        @pl.when(owner_z != z)
        def _():
            pltpu.make_async_remote_copy(
                src_ref=source,
                dst_ref=target_ref.at[z],
                send_sem=send_sem.at[index],
                recv_sem=recv_sem,
                device_id={"tok": owner_z},
                device_id_type=MESH,
            ).wait_send()

    def head_cols(index):
        return pl.ds(pl.multiple_of(index * HD, HD), HD)

    turns = (2, 3, 1, 4, 0)

    def spread(turn):
        return lax.rem(z // 3 + turn, heads_here)

    def key_part(side, index):
        return ks.at[0, side * half : (side + 1) * half, head_cols(index)]

    def send_keys():
        for index in map(spread, turns):
            for side in (0, 1):
                to_owner(key_part(side, index), k_all.at[side], k_send.at[side], k_recv, index)

    def send_queries():
        for index in map(spread, turns):
            to_owner(qs.at[0, :, head_cols(index)], q_all, q_send, q_recv.at[z], index)

    chunks = n_tok * rows // QCHUNK
    per_chunk = QCHUNK // rows

    def weigh(chunk):
        query = q_all[pl.ds(chunk * per_chunk, per_chunk)].reshape(QCHUNK, HD)
        key = k_all[...].reshape(n_tok * rows, HD)
        raw = lax.dot_general(key, query, NT, preferred_element_type=jnp.float32)
        top = jnp.max(raw, axis=0, keepdims=True)
        grown = jnp.exp2((raw - top) * (HD ** (-0.5) * LOG2E))
        total = jnp.sum(grown, axis=0, keepdims=True)
        cols = pl.ds(pl.multiple_of(chunk * QCHUNK, QCHUNK), QCHUNK)
        probs[:, cols] = (grown * (1.0 / total)).astype(jnp.bfloat16)

    def advance(step):
        for index in range(PIECES):
            for direction in (0, 1):
                count = reach(direction, index)

                @pl.when(step <= count)
                def _():
                    ring(direction, index, step - 1).wait_recv()

                @pl.when(step < count)
                def _():
                    ring(direction, index, step).start()

    def weigh_turn(turn):
        @pl.when(turn == 0)
        def _():
            pltpu.make_async_copy(k_all, k_all, k_recv).wait()

        shift = (turn + 1) // 2 * (2 * lax.rem(turn, 2) - 1)
        chunk = lax.rem(z // per_chunk + shift + chunks, chunks)
        for place in range(per_chunk):
            source = chunk * per_chunk + place
            view = q_all.at[source]
            pltpu.make_async_copy(view, view, q_recv.at[source]).wait()
        weigh(chunk)

    weighed = min(chunks, PER_STEP * (hops - WEIGH_AT))

    @pl.loop(1, hops + 1)
    def _(step):
        @pl.when(step == K_AT)
        def _():
            send_keys()

        @pl.when(step == Q_AT)
        def _():
            send_queries()

        advance(step)

        @pl.when(jnp.logical_and(owner, jnp.logical_and(step >= WEIGH_AT, step < hops)))
        def _():
            first = (step - WEIGH_AT) * PER_STEP

            @pl.loop(0, PER_STEP)
            def _(turn):
                pl.when(first + turn < weighed)(lambda: weigh_turn(first + turn))

    for step in range(1, n_head):
        to_mate(step).wait_recv()

    for index in map(spread, turns):
        total = None
        for source in range(n_head):
            term = jnp.dot(
                scaled[source],
                w_full[source * width : (source + 1) * width, head_cols(index)],
                preferred_element_type=jnp.float32,
            )
            total = term if total is None else total + term
        for branch in (0, 1):
            grad[branch, :, head_cols(index)] = total[branch * rows : (branch + 1) * rows].astype(
                jnp.bfloat16
            )
        to_owner(grad.at[0, :, head_cols(index)], g_all, g_send, g_recv, index)

    load_v.wait()

    def exchange(branch, side):
        return pltpu.make_async_remote_copy(
            src_ref=part.at[branch, side],
            dst_ref=part_in.at[branch, side],
            send_sem=p_send.at[branch, side],
            recv_sem=p_recv.at[branch, side],
            device_id={"head": mate},
            device_id_type=MESH,
        )

    def pair_down(branch, side, y):
        slot = (branch * 2 + side) * 2
        return hand_down(
            pair.at[branch, side, y],
            pair_in.at[branch, side, row_y],
            c_send.at[1 + slot + y],
            c_recv.at[1 + slot + row_y],
            2 * y + core,
        )

    def project(branch, side, value):
        def back(target):
            weight = v_full[pl.ds(pl.multiple_of(target * width, 128), width), :]
            return lax.dot_general(value, weight, NT, preferred_element_type=jnp.float32)

        for y in range(n_head // 2):
            part[branch, side, y] = back(2 * y + 1 - core).astype(jnp.bfloat16)
        exchange(branch, side).start()
        for y in range(n_head // 2):
            own[y] = back(2 * y + core)
        exchange(branch, side).wait_recv()
        for y in range(n_head // 2):
            total = own[y] + part_in[branch, side, y].astype(jnp.float32)
            pair[branch, side, y] = total.astype(jnp.bfloat16)
            pl.when(sends_down)(lambda: pair_down(branch, side, y).start())

    def collect(branch, side):
        @pl.when(takes_down)
        def _():
            for y in range(n_head // 2):
                slot = (branch * 2 + side) * 2 + y
                view = pair_in.at[branch, side, y]
                pltpu.make_async_copy(view, view, c_recv.at[1 + slot]).wait()
            span = slice(side * half, (side + 1) * half)
            total = held_next[branch, span, :].astype(jnp.float32)
            for y in range(n_head // 2):
                total = total + pair_in[branch, side, y].astype(jnp.float32)
            out[branch, span, :] = total.astype(jnp.bfloat16)

    own_cols = pl.ds(pl.multiple_of(my_head * HD, HD), HD)

    def back_to(side, block):
        return pltpu.make_async_remote_copy(
            src_ref=o_buf.at[side, block],
            dst_ref=vgrad.at[side, :, own_cols],
            send_sem=o_send.at[side, block],
            recv_sem=o_recv.at[side],
            device_id={"tok": block},
            device_id_type=MESH,
        )

    for side in (0, 1):
        project(1, side, grad[1, side * half : (side + 1) * half, :])

    together = 2 * rows // half

    @pl.when(owner)
    def _():
        @pl.loop(weighed, chunks)
        def _(turn):
            weigh_turn(turn)

        pltpu.make_async_copy(g_all, g_all, g_recv).wait()
        groups = n_tok // together

        for side in (0, 1):

            @pl.loop(0, groups)
            def _(turn):
                base = lax.rem(z // together + groups // 2 + turn, groups) * together
                start = pl.multiple_of((side * n_tok + base) * half, together * half)
                several = jnp.dot(
                    probs[pl.ds(start, together * half), :],
                    g_all[...].reshape(n_tok * rows, HD),
                    preferred_element_type=jnp.float32,
                ).astype(jnp.bfloat16)
                for place in range(together):
                    block = base + place
                    o_buf[side, block] = several[place * half : (place + 1) * half]

                    @pl.when(block == z)
                    def _():
                        pltpu.make_async_copy(
                            o_buf.at[side, block], vgrad.at[side, :, own_cols], o_recv.at[side]
                        ).start()

                    @pl.when(block != z)
                    def _():
                        back_to(side, block).start()

    @pl.when(takes_down)
    def _():
        pltpu.make_async_copy(held_next, held_next, c_recv.at[0]).wait()

    @pl.when(jnp.logical_not(takes_down))
    def _():
        out[...] = jnp.zeros_like(out)

    for side in (0, 1):
        collect(1, side)
    for side in (0, 1):
        pltpu.make_async_copy(vgrad.at[side], vgrad.at[side], o_recv.at[side]).wait()
        project(0, side, vgrad[side])
    for side in (0, 1):
        collect(0, side)

    for index in range(heads_here):
        for side in (0, 1):
            wait_to_owner(key_part(side, index), k_all.at[side], k_send.at[side], k_recv, index)
        wait_to_owner(qs.at[0, :, head_cols(index)], q_all, q_send, q_recv.at[z], index)
        wait_to_owner(grad.at[0, :, head_cols(index)], g_all, g_send, g_recv, index)

    for index in range(PIECES):
        for direction in (0, 1):

            @pl.loop(0, reach(direction, index))
            def _(step):
                ring(direction, index, step).wait_send()

    @pl.when(owner)
    def _():
        for side in (0, 1):

            @pl.loop(0, n_tok)
            def _(block):
                @pl.when(block != z)
                def _():
                    back_to(side, block).wait_send()

    for step in range(1, n_head):
        to_mate(step).wait_send()
    for branch in (0, 1):
        for side in (0, 1):
            exchange(branch, side).wait_send()

    @pl.when(sends_down)
    def _():
        held_copy().wait_send()
        for branch in (0, 1):
            for side in (0, 1):
                for y in range(n_head // 2):
                    pair_down(branch, side, y).wait_send()


def shards(
    sizes,
    held_cotangents,
    entering_adjoint,
    saved_queries,
    saved_keys,
    value_weight,
    out_weight,
    block_gate,
    time_gate,
    timestep,
):
    n_sec, n_head, n_tok = sizes
    _, branches, rows, width = held_cotangents.shape
    heads_here = width // HD
    model = block_gate.shape[1]
    tokens = n_tok * rows
    bf16 = jnp.bfloat16
    dma = pltpu.SemaphoreType.DMA
    anywhere = pl.BlockSpec(memory_space=pl.ANY)
    vmem = pl.BlockSpec(memory_space=pltpu.VMEM)
    passed_on = pl.pallas_call(
        functools.partial(kernel, n_sec, n_head, n_tok),
        out_shape=jax.ShapeDtypeStruct((branches, rows, width), bf16),
        in_specs=[anywhere] * 5 + [vmem, vmem, pl.BlockSpec(memory_space=pltpu.SMEM)],
        out_specs=vmem,
        scratch_shapes=[
            pltpu.VMEM((branches, rows, width), bf16),
            pltpu.VMEM((n_head, branches * rows, width), bf16),
            pltpu.VMEM((model, width), bf16),
            pltpu.VMEM((model, width), bf16),
            pltpu.VMEM((n_tok, rows, HD), bf16),
            pltpu.VMEM((2, n_tok, rows // 2, HD), bf16),
            pltpu.VMEM((n_tok, rows, HD), bf16),
            pltpu.VMEM((tokens, tokens), bf16),
            pltpu.VMEM((branches, rows, width), bf16),
            pltpu.VMEM((2, n_tok, rows // 2, HD), bf16),
            pltpu.VMEM((2, rows // 2, width), bf16),
            pltpu.VMEM((branches, 2, n_head // 2, rows // 2, width), bf16),
            pltpu.VMEM((branches, 2, n_head // 2, rows // 2, width), bf16),
            pltpu.VMEM((n_head // 2, rows // 2, width), jnp.float32),
            pltpu.VMEM((branches, 2, n_head // 2, rows // 2, width), bf16),
            pltpu.VMEM((branches, 2, n_head // 2, rows // 2, width), bf16),
            pltpu.VMEM((branches, rows, width), bf16),
            dma((3,)),
            dma((n_head - 1,)),
            dma((n_head - 1,)),
            dma((2, PIECES, n_tok // 2)),
            dma((2, PIECES, n_tok // 2)),
            dma((heads_here,)),
            dma((n_tok,)),
            dma((2, heads_here)),
            dma,
            dma((heads_here,)),
            dma,
            dma((2, n_tok)),
            dma((2,)),
            dma((branches, 2)),
            dma((branches, 2)),
            dma((9,)),
            dma((9,)),
        ],
        compiler_params=pltpu.CompilerParams(
            collective_id=0, has_side_effects=True, vmem_limit_bytes=56 * 1024 * 1024
        ),
        name="tick",
    )(
        held_cotangents,
        saved_queries,
        saved_keys,
        value_weight,
        out_weight,
        block_gate,
        time_gate,
        timestep,
    )
    entering_full = entering_adjoint.astype(jnp.float32)
    fresh_rows = jnp.stack([(1.0 + GUIDE) * entering_full, -GUIDE * entering_full]).astype(bf16)
    is_last = lax.axis_index("section") == n_sec - 1
    return jnp.where(is_last, fresh_rows, passed_on)[None]


def solution(mesh):
    sizes = (mesh.shape["section"], mesh.shape["head"], mesh.shape["tok"])
    return jax.shard_map(
        functools.partial(shards, sizes),
        mesh=mesh,
        in_specs=(
            P("section", None, "tok", "head"),
            P("tok", "head"),
            P("section", "tok", "head"),
            P("section", "tok", "head"),
            P("section", None, "head"),
            P("section", "tok", "head"),
            P("section", None),
            P(),
            P(),
        ),
        out_specs=P("section", None, "tok", "head"),
        check_vma=False,
    )
```

```python
import functools

import jax
import jax.numpy as jnp
from jax import lax
from jax.experimental import pallas as pl
from jax.experimental.pallas import tpu as pltpu
from jax.sharding import PartitionSpec as P

HD = 128
GUIDE = 3.0
MESH = pl.DeviceIdType.MESH
LOG2E = 1.4426950408889634
NT = (((1,), (1,)), ((), ()))
QCHUNK = 256
PIECES = 5
K_AT = 2
Q_AT = 2
VOUCH_FIRST = 4
WEIGH_AT = 4
PER_STEP = 2


def kernel(
    n_sec,
    n_head,
    n_tok,
    held,
    qs,
    ks,
    vw,
    ow,
    bgate,
    tgate,
    tstep,
    out,
    held_v,
    scaled,
    w_full,
    v_full,
    q_all,
    k_all,
    g_all,
    probs,
    grad,
    o_buf,
    vgrad,
    part,
    part_in,
    own,
    pair,
    pair_in,
    held_next,
    enter_sem,
    load_sem,
    a_send,
    a_recv,
    r_send,
    r_recv,
    q_send,
    q_recv,
    k_send,
    k_recv,
    g_send,
    g_recv,
    o_send,
    o_recv,
    p_send,
    p_recv,
    c_send,
    c_recv,
):
    sec, head, z = lax.axis_index("section"), lax.axis_index("head"), lax.axis_index("tok")
    core = lax.rem(head, 2)
    width = held.shape[3]
    rows = held.shape[2]
    heads_here = width // HD
    wrows = ow.shape[1]
    piece_rows = wrows // PIECES
    hops = n_tok // 2
    half = rows // 2
    mate = head + 1 - 2 * core
    row_y = head // 2
    right, left = lax.rem(z + 1, n_tok), lax.rem(z + n_tok - 1, n_tok)
    my_head = z // 3
    owner = jnp.logical_and(lax.rem(z, 3) == core, z < 3 * heads_here)

    load_held = pltpu.make_async_copy(held.at[0], held_v, load_sem.at[0])
    load_held.start()
    load_w = pltpu.make_async_copy(
        ow.at[0], w_full.at[pl.ds(pl.multiple_of(z * wrows, 16), wrows), :], load_sem.at[1]
    )
    load_w.start()
    load_v = pltpu.make_async_copy(vw.at[0], v_full, load_sem.at[2])
    load_v.start()

    barrier = pltpu.get_barrier_semaphore()
    for neighbour in (left, right):
        pl.semaphore_signal(barrier, inc=1, device_id={"tok": neighbour}, device_id_type=MESH)
    for step in range(1, n_head):
        pl.semaphore_signal(
            barrier, inc=1, device_id={"head": lax.rem(head + step, n_head)}, device_id_type=MESH
        )
    for step in (1, n_sec - 1):
        for turn in (0, 2):
            pl.semaphore_signal(
                barrier,
                inc=1,
                device_id={
                    "section": lax.rem(sec + step, n_sec),
                    "head": lax.rem(head + turn, n_head),
                },
                device_id_type=MESH,
            )
    pl.semaphore_wait(barrier, 2 + n_head - 1 + 4)

    def vouch(levels):
        for _ in range(levels):
            pl.semaphore_signal(
                enter_sem.at[0], inc=1, device_id={"tok": right}, device_id_type=MESH
            )
            pl.semaphore_signal(enter_sem.at[1], inc=1, device_id={"tok": left}, device_id_type=MESH)
            for side in (0, 1):
                pl.semaphore_wait(enter_sem.at[side], 1)


    def ring(direction, index, step):
        block = lax.rem(z + n_tok - step, n_tok) if direction == 0 else lax.rem(z + step, n_tok)
        start = pl.multiple_of(block * wrows + index * piece_rows, 16)
        view = w_full.at[pl.ds(start, piece_rows), :]
        return pltpu.make_async_remote_copy(
            src_ref=view,
            dst_ref=view,
            send_sem=r_send.at[direction, index, step],
            recv_sem=r_recv.at[direction, index, step],
            device_id={"tok": right if direction == 0 else left},
            device_id_type=MESH,
        )

    def reach(direction, index):
        return hops - (direction + index) % 2

    load_w.wait()
    for index in range(PIECES):
        for direction in (0, 1):
            ring(direction, index, 0).start()

    time_row = jnp.sum(
        jnp.where(
            lax.broadcasted_iota(jnp.int32, (tgate.shape[0], width), 0) == tstep[0],
            tgate[:, pl.ds(pl.multiple_of(head * width, 128), width)],
            0.0,
        ),
        axis=0,
        keepdims=True,
    )
    gate_row = bgate[:, pl.ds(pl.multiple_of(head * width, 128), width)] + time_row
    load_held.wait()
    for branch in (0, 1):
        scaled[head, branch * rows : (branch + 1) * rows, :] = (
            held_v[branch].astype(jnp.float32) * gate_row
        ).astype(jnp.bfloat16)

    def to_mate(step):
        return pltpu.make_async_remote_copy(
            src_ref=scaled.at[head],
            dst_ref=scaled.at[head],
            send_sem=a_send.at[step - 1],
            recv_sem=a_recv.at[step - 1],
            device_id={"head": lax.rem(head + step, n_head)},
            device_id_type=MESH,
        )

    for step in range(1, n_head):
        to_mate(step).start()

    def hand_down(source, target, send_sem, recv_sem, head_index):
        return pltpu.make_async_remote_copy(
            src_ref=source,
            dst_ref=target,
            send_sem=send_sem,
            recv_sem=recv_sem,
            device_id={"section": lax.rem(sec + n_sec - 1, n_sec), "head": head_index},
            device_id_type=MESH,
        )

    def held_copy():
        return hand_down(held_v, held_next, c_send.at[0], c_recv.at[0], head)

    sends_down = sec > 0
    takes_down = sec < n_sec - 1
    pl.when(sends_down)(lambda: held_copy().start())

    def to_owner(source, target_ref, send_sem, recv_sem, index):
        owner_z = 3 * index + core

        @pl.when(owner_z == z)
        def _():
            pltpu.make_async_copy(source, target_ref.at[z], recv_sem).start()

        @pl.when(owner_z != z)
        def _():
            pltpu.make_async_remote_copy(
                src_ref=source,
                dst_ref=target_ref.at[z],
                send_sem=send_sem.at[index],
                recv_sem=recv_sem,
                device_id={"tok": owner_z},
                device_id_type=MESH,
            ).start()

    def wait_to_owner(source, target_ref, send_sem, recv_sem, index):
        owner_z = 3 * index + core

        @pl.when(owner_z != z)
        def _():
            pltpu.make_async_remote_copy(
                src_ref=source,
                dst_ref=target_ref.at[z],
                send_sem=send_sem.at[index],
                recv_sem=recv_sem,
                device_id={"tok": owner_z},
                device_id_type=MESH,
            ).wait_send()

    def head_cols(index):
        return pl.ds(pl.multiple_of(index * HD, HD), HD)

    turns = (2, 3, 1, 4, 0)

    def spread(turn):
        return lax.rem(z // 3 + turn, heads_here)

    def key_part(side, index):
        return ks.at[0, side * half : (side + 1) * half, head_cols(index)]

    def send_keys():
        for index in map(spread, turns):
            for side in (0, 1):
                to_owner(key_part(side, index), k_all.at[side], k_send.at[side], k_recv, index)

    def send_queries():
        for index in map(spread, turns):
            to_owner(qs.at[0, :, head_cols(index)], q_all, q_send, q_recv.at[z], index)

    chunks = n_tok * rows // QCHUNK
    per_chunk = QCHUNK // rows

    def weigh(chunk):
        query = q_all[pl.ds(chunk * per_chunk, per_chunk)].reshape(QCHUNK, HD)
        key = k_all[...].reshape(n_tok * rows, HD)
        raw = lax.dot_general(key, query, NT, preferred_element_type=jnp.float32) * (
            HD ** (-0.5) * LOG2E
        )
        top = jnp.max(raw, axis=0, keepdims=True)
        grown = jnp.exp2(raw - top)
        total = jnp.sum(grown, axis=0, keepdims=True)
        cols = pl.ds(pl.multiple_of(chunk * QCHUNK, QCHUNK), QCHUNK)
        probs[:, cols] = (grown * (1.0 / total)).astype(jnp.bfloat16)

    def advance(step):
        for index in range(PIECES):
            for direction in (0, 1):
                count = reach(direction, index)

                @pl.when(step <= count)
                def _():
                    ring(direction, index, step - 1).wait_recv()

                @pl.when(step < count)
                def _():
                    ring(direction, index, step).start()

    def weigh_turn(turn):
        @pl.when(turn == 0)
        def _():
            pltpu.make_async_copy(k_all, k_all, k_recv).wait()

        shift = (turn + 1) // 2 * (2 * lax.rem(turn, 2) - 1)
        chunk = lax.rem(z // per_chunk + shift + chunks, chunks)
        for place in range(per_chunk):
            source = chunk * per_chunk + place
            view = q_all.at[source]
            pltpu.make_async_copy(view, view, q_recv.at[source]).wait()
        weigh(chunk)

    weighed = min(chunks, PER_STEP * (hops - WEIGH_AT))

    vouch(VOUCH_FIRST)

    @pl.loop(1, hops + 1)
    def _(step):
        @pl.when(step == K_AT)
        def _():
            vouch(hops - 1 - VOUCH_FIRST)
            send_keys()

        @pl.when(step == Q_AT)
        def _():
            send_queries()

        advance(step)

        @pl.when(jnp.logical_and(owner, jnp.logical_and(step >= WEIGH_AT, step < hops)))
        def _():
            first = (step - WEIGH_AT) * PER_STEP

            @pl.loop(0, PER_STEP)
            def _(turn):
                pl.when(first + turn < weighed)(lambda: weigh_turn(first + turn))

    for step in range(1, n_head):
        to_mate(step).wait_recv()

    for index in map(spread, turns):
        total = None
        for source in range(n_head):
            term = jnp.dot(
                scaled[source],
                w_full[source * width : (source + 1) * width, head_cols(index)],
                preferred_element_type=jnp.float32,
            )
            total = term if total is None else total + term
        for branch in (0, 1):
            grad[branch, :, head_cols(index)] = total[branch * rows : (branch + 1) * rows].astype(
                jnp.bfloat16
            )
        to_owner(grad.at[0, :, head_cols(index)], g_all, g_send, g_recv, index)

    load_v.wait()

    def exchange(branch, side):
        return pltpu.make_async_remote_copy(
            src_ref=part.at[branch, side],
            dst_ref=part_in.at[branch, side],
            send_sem=p_send.at[branch, side],
            recv_sem=p_recv.at[branch, side],
            device_id={"head": mate},
            device_id_type=MESH,
        )

    def pair_down(branch, side, y):
        slot = (branch * 2 + side) * 2
        return hand_down(
            pair.at[branch, side, y],
            pair_in.at[branch, side, row_y],
            c_send.at[1 + slot + y],
            c_recv.at[1 + slot + row_y],
            2 * y + core,
        )

    def project(branch, side, value):
        def back(target):
            weight = v_full[pl.ds(pl.multiple_of(target * width, 128), width), :]
            return lax.dot_general(value, weight, NT, preferred_element_type=jnp.float32)

        for y in range(n_head // 2):
            part[branch, side, y] = back(2 * y + 1 - core).astype(jnp.bfloat16)
        exchange(branch, side).start()
        for y in range(n_head // 2):
            own[y] = back(2 * y + core)
        exchange(branch, side).wait_recv()
        for y in range(n_head // 2):
            total = own[y] + part_in[branch, side, y].astype(jnp.float32)
            pair[branch, side, y] = total.astype(jnp.bfloat16)
            pl.when(sends_down)(lambda: pair_down(branch, side, y).start())

    def collect(branch, side):
        @pl.when(takes_down)
        def _():
            for y in range(n_head // 2):
                slot = (branch * 2 + side) * 2 + y
                view = pair_in.at[branch, side, y]
                pltpu.make_async_copy(view, view, c_recv.at[1 + slot]).wait()
            span = slice(side * half, (side + 1) * half)
            total = held_next[branch, span, :].astype(jnp.float32)
            for y in range(n_head // 2):
                total = total + pair_in[branch, side, y].astype(jnp.float32)
            out[branch, span, :] = total.astype(jnp.bfloat16)

    own_cols = pl.ds(pl.multiple_of(my_head * HD, HD), HD)

    def back_to(side, block):
        return pltpu.make_async_remote_copy(
            src_ref=o_buf.at[side, block],
            dst_ref=vgrad.at[side, :, own_cols],
            send_sem=o_send.at[side, block],
            recv_sem=o_recv.at[side],
            device_id={"tok": block},
            device_id_type=MESH,
        )

    for side in (0, 1):
        project(1, side, grad[1, side * half : (side + 1) * half, :])

    together = 2 * rows // half

    @pl.when(owner)
    def _():
        @pl.loop(weighed, chunks)
        def _(turn):
            weigh_turn(turn)

        pltpu.make_async_copy(g_all, g_all, g_recv).wait()
        groups = n_tok // together

        for side in (0, 1):

            @pl.loop(0, groups)
            def _(turn):
                base = lax.rem(z // together + groups // 2 + turn, groups) * together
                start = pl.multiple_of((side * n_tok + base) * half, together * half)
                several = jnp.dot(
                    probs[pl.ds(start, together * half), :],
                    g_all[...].reshape(n_tok * rows, HD),
                    preferred_element_type=jnp.float32,
                ).astype(jnp.bfloat16)
                for place in range(together):
                    block = base + place
                    o_buf[side, block] = several[place * half : (place + 1) * half]

                    @pl.when(block == z)
                    def _():
                        pltpu.make_async_copy(
                            o_buf.at[side, block], vgrad.at[side, :, own_cols], o_recv.at[side]
                        ).start()

                    @pl.when(block != z)
                    def _():
                        back_to(side, block).start()

    @pl.when(takes_down)
    def _():
        pltpu.make_async_copy(held_next, held_next, c_recv.at[0]).wait()

    @pl.when(jnp.logical_not(takes_down))
    def _():
        out[...] = jnp.zeros_like(out)

    for side in (0, 1):
        collect(1, side)
    for side in (0, 1):
        pltpu.make_async_copy(vgrad.at[side], vgrad.at[side], o_recv.at[side]).wait()
        project(0, side, vgrad[side])
    for side in (0, 1):
        collect(0, side)

    for index in range(heads_here):
        for side in (0, 1):
            wait_to_owner(key_part(side, index), k_all.at[side], k_send.at[side], k_recv, index)
        wait_to_owner(qs.at[0, :, head_cols(index)], q_all, q_send, q_recv.at[z], index)
        wait_to_owner(grad.at[0, :, head_cols(index)], g_all, g_send, g_recv, index)

    for index in range(PIECES):
        for direction in (0, 1):

            @pl.loop(0, reach(direction, index))
            def _(step):
                ring(direction, index, step).wait_send()

    @pl.when(owner)
    def _():
        for side in (0, 1):

            @pl.loop(0, n_tok)
            def _(block):
                @pl.when(block != z)
                def _():
                    back_to(side, block).wait_send()

    for step in range(1, n_head):
        to_mate(step).wait_send()
    for branch in (0, 1):
        for side in (0, 1):
            exchange(branch, side).wait_send()

    @pl.when(sends_down)
    def _():
        held_copy().wait_send()
        for branch in (0, 1):
            for side in (0, 1):
                for y in range(n_head // 2):
                    pair_down(branch, side, y).wait_send()


def shards(
    sizes,
    held_cotangents,
    entering_adjoint,
    saved_queries,
    saved_keys,
    value_weight,
    out_weight,
    block_gate,
    time_gate,
    timestep,
):
    n_sec, n_head, n_tok = sizes
    _, branches, rows, width = held_cotangents.shape
    heads_here = width // HD
    model = block_gate.shape[1]
    tokens = n_tok * rows
    bf16 = jnp.bfloat16
    dma = pltpu.SemaphoreType.DMA
    anywhere = pl.BlockSpec(memory_space=pl.ANY)
    vmem = pl.BlockSpec(memory_space=pltpu.VMEM)
    passed_on = pl.pallas_call(
        functools.partial(kernel, n_sec, n_head, n_tok),
        out_shape=jax.ShapeDtypeStruct((branches, rows, width), bf16),
        in_specs=[anywhere] * 5 + [vmem, vmem, pl.BlockSpec(memory_space=pltpu.SMEM)],
        out_specs=vmem,
        scratch_shapes=[
            pltpu.VMEM((branches, rows, width), bf16),
            pltpu.VMEM((n_head, branches * rows, width), bf16),
            pltpu.VMEM((model, width), bf16),
            pltpu.VMEM((model, width), bf16),
            pltpu.VMEM((n_tok, rows, HD), bf16),
            pltpu.VMEM((2, n_tok, rows // 2, HD), bf16),
            pltpu.VMEM((n_tok, rows, HD), bf16),
            pltpu.VMEM((tokens, tokens), bf16),
            pltpu.VMEM((branches, rows, width), bf16),
            pltpu.VMEM((2, n_tok, rows // 2, HD), bf16),
            pltpu.VMEM((2, rows // 2, width), bf16),
            pltpu.VMEM((branches, 2, n_head // 2, rows // 2, width), bf16),
            pltpu.VMEM((branches, 2, n_head // 2, rows // 2, width), bf16),
            pltpu.VMEM((n_head // 2, rows // 2, width), jnp.float32),
            pltpu.VMEM((branches, 2, n_head // 2, rows // 2, width), bf16),
            pltpu.VMEM((branches, 2, n_head // 2, rows // 2, width), bf16),
            pltpu.VMEM((branches, rows, width), bf16),
            pltpu.SemaphoreType.REGULAR((2,)),
            dma((3,)),
            dma((n_head - 1,)),
            dma((n_head - 1,)),
            dma((2, PIECES, n_tok // 2)),
            dma((2, PIECES, n_tok // 2)),
            dma((heads_here,)),
            dma((n_tok,)),
            dma((2, heads_here)),
            dma,
            dma((heads_here,)),
            dma,
            dma((2, n_tok)),
            dma((2,)),
            dma((branches, 2)),
            dma((branches, 2)),
            dma((9,)),
            dma((9,)),
        ],
        compiler_params=pltpu.CompilerParams(
            collective_id=0, has_side_effects=True, vmem_limit_bytes=56 * 1024 * 1024
        ),
        name="tick",
    )(
        held_cotangents,
        saved_queries,
        saved_keys,
        value_weight,
        out_weight,
        block_gate,
        time_gate,
        timestep,
    )
    entering_full = entering_adjoint.astype(jnp.float32)
    fresh_rows = jnp.stack([(1.0 + GUIDE) * entering_full, -GUIDE * entering_full]).astype(bf16)
    is_last = lax.axis_index("section") == n_sec - 1
    return jnp.where(is_last, fresh_rows, passed_on)[None]


def solution(mesh):
    sizes = (mesh.shape["section"], mesh.shape["head"], mesh.shape["tok"])
    return jax.shard_map(
        functools.partial(shards, sizes),
        mesh=mesh,
        in_specs=(
            P("section", None, "tok", "head"),
            P("tok", "head"),
            P("section", "tok", "head"),
            P("section", "tok", "head"),
            P("section", None, "head"),
            P("section", "tok", "head"),
            P("section", None),
            P(),
            P(),
        ),
        out_specs=P("section", None, "tok", "head"),
        check_vma=False,
    )
```
